32 devices in a mesh: dp: 2 (over x), ctx: 4 (over y, core), tensor: 4 (over z).
Axes of the slice: x: 2, y: 2, z: 4, core: 2. Of those that a mesh axis runs over, the one named last changes fastest.
Arguments:
- hidden: bfloat16 [2, 16384, 2560], P('dp', 'ctx', 'tensor'), may hold values from -6 to 6
- depth: int32 [2, 16384], P('dp', 'ctx'), may hold values from 1 to 4, as said below
- qkv_weight: bfloat16 [2560, 3, 2560], P(None, None, 'tensor'), may hold values from -0.125 to 0.125
- out_weight: bfloat16 [2560, 2560], P('tensor'), may hold values from -0.125 to 0.125
Outputs:
- update: bfloat16 [2, 16384, 2560], P('dp', 'ctx', 'tensor')
The draws below stay inside these ranges and needn't reach their ends.
Inputs may be any that keep to these rules, and one draw needn't show every extreme that they name: In every aligned block of 4096 positions of a document at most 1024 tokens have depth at least 3, and some block has exactly 1024; over all documents exactly 4096 tokens do.
All inputs are finite; a program needn't handle non-finite values.
Results may differ from the reference program's by a relative error of at most 0.012.
The reference program's roundings to bfloat16 on the way count: a program that leaves them out, or rounds other values in their place, can miss the bound.
Values may be sent and summed in bfloat16 or wider, within the bound.
A program may use at most 256 MiB of HBM per device.

```python
import jax
import jax.numpy as jnp
from jax import lax

D = 2560
HEADS = 20
HD = 128
RECURSION = 3
MAX_DEPTH = 4
TOK_DEV = 4096
ACT_DEV = 512
CAP = 1024
DOCS = 2
LEN = 16384
N_DP = 2
N_CTX = 4
N_TENSOR = 4


def draw_depth(key, part):
    shard_total = DOCS * (LEN // TOK_DEV)
    half_total = shard_total // 2
    key_order, key_load, key_place, key_deep, key_shallow = jax.random.split(jax.random.fold_in(key, 17), 5)
    loads = jax.random.randint(key_load, (half_total,), 0, CAP + 1)
    loads = loads.at[0].set(CAP)
    paired = jnp.concatenate([loads, CAP - loads])
    shuffled = jax.random.permutation(key_order, shard_total)
    shard_counts = jnp.zeros((shard_total,), jnp.int32).at[shuffled].set(paired.astype(jnp.int32))
    place_keys = jax.random.split(key_place, shard_total)
    ranking = jax.vmap(lambda single: jax.random.permutation(single, TOK_DEV))(place_keys)
    chosen = ranking < shard_counts[:, None]
    deeper = jax.random.randint(key_deep, (shard_total, TOK_DEV), RECURSION, MAX_DEPTH + 1)
    shallow = jax.random.randint(key_shallow, (shard_total, TOK_DEV), 1, RECURSION)
    return jnp.where(chosen, deeper, shallow).reshape(DOCS, LEN).astype(jnp.int32)


def levels(rng, shape, cuts, low, largest):
    def one(axis_at, parts):
        draws = jax.random.uniform(jax.random.fold_in(jax.random.fold_in(rng, 6), axis_at), (parts,), jnp.float32, low / len(cuts), largest / len(cuts))
        return jnp.repeat(jnp.exp(draws), shape[axis_at] // parts).reshape((-1,) + (1,) * (len(shape) - axis_at - 1))

    factor_of = one(*cuts[0])
    for cut in cuts[1:]:
        factor_of = factor_of * one(*cut)
    return factor_of


def bell_draw(stream_key, shape, scale, limit, pieces=(), kind=jnp.bfloat16):
    array = scale * jax.random.normal(stream_key, shape, jnp.float32)
    if pieces:
        array = array * levels(stream_key, shape, pieces, -0.22, 0.18)
    return jnp.clip(array, -limit, limit).astype(kind)


def setup_inputs(seed: int = 0) -> dict:
    streams_of = jax.random.split(jax.random.key(seed), 5)
    return {
        "hidden": bell_draw(streams_of[0], (DOCS, LEN, D), 1.0, 6.0, ((0, 2), (1, 4), (2, 4))),
        "depth": draw_depth(jax.random.fold_in(streams_of[4], 71), 0),
        "qkv_weight": bell_draw(streams_of[2], (D, 3, HEADS * HD), D ** -0.5, 0.125, ((2, 4),)),
        "out_weight": bell_draw(streams_of[3], (HEADS * HD, D), (HEADS * HD) ** -0.5, 0.125, ((0, 4),)),
    }


score_scale = 0.25
norm_epsilon = 1e-05
head_epsilon = 1e-06

def head_normed(values):
    row_count = values.shape[0]
    per_head = values.reshape(row_count, -1, HD)
    factor = lax.rsqrt(lax.optimization_barrier(jnp.mean(per_head * per_head, axis=2, keepdims=True)) + head_epsilon)
    return (per_head * factor).reshape(row_count, -1).astype(jnp.bfloat16)

def reference(hidden, depth, qkv_weight, out_weight):
    doc_total, length, feature_width = hidden.shape
    head_width = qkv_weight.shape[2]
    active_total = ACT_DEV * N_DP * N_CTX
    doc_room = min(length, N_CTX * CAP)
    active = depth >= RECURSION
    doc_counts = lax.optimization_barrier(jnp.sum(active.astype(jnp.int32), axis=1)).astype(jnp.int32)
    doc_starts = (jnp.cumsum(doc_counts) - doc_counts).astype(jnp.int32)
    flat_index = jnp.nonzero(active.reshape(-1), size=active_total, fill_value=0)[0].astype(jnp.int32)
    token_rows = hidden.reshape(-1, feature_width)[flat_index].astype(jnp.float32)
    factor = lax.rsqrt(lax.optimization_barrier(jnp.mean(token_rows * token_rows, axis=1, keepdims=True)) + norm_epsilon)
    normed = (token_rows * factor).astype(jnp.bfloat16)
    projection = jnp.dot(normed, qkv_weight.reshape(feature_width, 3 * head_width), preferred_element_type=jnp.float32)
    queries = head_normed(projection[:, :head_width])
    key_rows = head_normed(projection[:, head_width:2 * head_width])
    value_rows = projection[:, 2 * head_width:].astype(jnp.bfloat16)
    positions = (flat_index % length).astype(jnp.int32)
    doc_of = (flat_index // length).astype(jnp.int32)
    padding = jnp.zeros((doc_room, head_width), jnp.bfloat16)
    padded_queries = jnp.concatenate([queries, padding], axis=0)
    padded_keys = jnp.concatenate([key_rows, padding], axis=0)
    padded_values = jnp.concatenate([value_rows, padding], axis=0)
    padded_positions = jnp.concatenate([positions, jnp.zeros((doc_room,), jnp.int32)], axis=0)

    def one_document(doc_number):
        doc_begin = doc_starts[doc_number]
        query_block = lax.dynamic_slice_in_dim(padded_queries, doc_begin, doc_room).astype(jnp.float32).reshape(doc_room, -1, HD)
        key_block = lax.dynamic_slice_in_dim(padded_keys, doc_begin, doc_room).astype(jnp.float32).reshape(doc_room, -1, HD)
        value_block = lax.dynamic_slice_in_dim(padded_values, doc_begin, doc_room).astype(jnp.float32).reshape(doc_room, -1, HD)
        position_block = lax.dynamic_slice_in_dim(padded_positions, doc_begin, doc_room)
        filled = jnp.arange(doc_room, dtype=jnp.int32) < doc_counts[doc_number]
        allowed = filled[:, None] & filled[None, :] & (position_block[None, :] <= position_block[:, None])
        scores = jnp.einsum('qhd,khd->hqk', query_block, key_block) * score_scale
        weights = jnp.where(allowed[None], jnp.exp(scores), 0.0)
        rounded = lax.optimization_barrier(weights.astype(jnp.bfloat16)).astype(jnp.float32)
        numerator = jnp.einsum('hqk,khd->qhd', rounded, value_block)
        denominator = lax.optimization_barrier(jnp.sum(weights, axis=2)) + (1.0 - filled.astype(jnp.float32))[None, :]
        context = numerator / jnp.transpose(denominator)[:, :, None]
        return context.reshape(doc_room, head_width).astype(jnp.bfloat16)
    contexts = lax.map(one_document, jnp.arange(doc_total, dtype=jnp.int32))
    within = (jnp.arange(active_total, dtype=jnp.int32) - doc_starts[doc_of]).astype(jnp.int32)
    context_rows = contexts[doc_of, within]
    group_width = head_width // N_TENSOR
    summed = jnp.zeros((active_total, feature_width), jnp.float32)
    for group_index in range(N_TENSOR):
        lower = group_index * group_width
        partial_value = jnp.dot(context_rows[:, lower:lower + group_width], out_weight[lower:lower + group_width], preferred_element_type=jnp.float32).astype(jnp.bfloat16)
        summed = summed + lax.optimization_barrier(partial_value).astype(jnp.float32)
    update = jnp.zeros((doc_total * length, feature_width), jnp.bfloat16).at[flat_index].set(summed.astype(jnp.bfloat16))
    return update.reshape(doc_total, length, feature_width)
```

```python
import functools

import jax
import jax.numpy as jnp
from jax import lax
from jax.experimental import pallas as pl
from jax.experimental.pallas import tpu as pltpu
from jax.sharding import PartitionSpec as P

HD = 128
RECURSION = 3
CAP = 1024
ACT_DEV = 512

score_scale = 0.25
norm_epsilon = 1e-05
head_epsilon = 1e-06
VMEM_LIMIT = 60 * 1024 * 1024
PLANE = ("dp", "ctx")


def project_kernel(x_ref, w_ref, o_ref, normed):
    part = pl.program_id(0)
    shards, rows, width = x_ref.shape

    @pl.when(part == 0)
    def _():
        total = jnp.zeros((rows, 1), jnp.float32)
        for z in range(shards):
            wide = x_ref[z].astype(jnp.float32)
            total = total + jnp.sum(wide * wide, axis=1, keepdims=True)
        factor = lax.rsqrt(total / (shards * width) + norm_epsilon)
        for z in range(shards):
            normed[z] = (x_ref[z].astype(jnp.float32) * factor).astype(jnp.bfloat16)

    acc = jnp.dot(normed[0], w_ref[0, :width], preferred_element_type=jnp.float32)
    for z in range(1, shards):
        acc = acc + jnp.dot(normed[z], w_ref[0, z * width : (z + 1) * width], preferred_element_type=jnp.float32)
    scale = jnp.where(part == 0, score_scale, 1.0)
    for h in range(acc.shape[1] // HD):
        head = acc[:, h * HD : (h + 1) * HD]
        factor = lax.rsqrt(jnp.mean(head * head, axis=1, keepdims=True) + head_epsilon) * scale
        factor = jnp.where(part == 2, 1.0, factor)
        o_ref[0, :, h * HD : (h + 1) * HD] = (head * factor).astype(jnp.bfloat16)


def project(rows_all, weight):
    shards, rows, width = rows_all.shape
    head_width = weight.shape[2]
    return pl.pallas_call(
        project_kernel,
        grid=(3,),
        out_shape=jax.ShapeDtypeStruct((3, rows, head_width), jnp.bfloat16),
        in_specs=[
            pl.BlockSpec((shards, rows, width), lambda p: (0, 0, 0)),
            pl.BlockSpec((1, shards * width, head_width), lambda p: (p, 0, 0)),
        ],
        out_specs=pl.BlockSpec((1, rows, head_width), lambda p: (p, 0, 0)),
        scratch_shapes=[pltpu.VMEM((shards, rows, width), jnp.bfloat16)],
        compiler_params=pltpu.CompilerParams(vmem_limit_bytes=VMEM_LIMIT),
        name="project",
    )(rows_all, weight)


def attend_kernel(docs, meta_ref, q_ref, k_ref, v_ref, o_ref):
    stripe = pl.program_id(1)
    plane, stripes, size, _ = k_ref.shape
    period = plane * size
    me = meta_ref[docs]
    query = q_ref[...]
    q_index = stripe * period + me * size + lax.broadcasted_iota(jnp.int32, (size, 1), 0)
    begin = jnp.zeros((size, 1), jnp.int32)
    for d in range(docs):
        begin = jnp.where(q_index >= meta_ref[d], meta_ref[d], begin)
    lane = lax.broadcasted_iota(jnp.int32, (size, period), 1)

    def tile(at, carry, diagonal):
        num, den = carry
        keys = k_ref[:, pl.ds(at, 1)].reshape(period, HD)
        values = v_ref[:, pl.ds(at, 1)].reshape(period, HD)
        scores = lax.dot_general(query, keys, (((1,), (1,)), ((), ())), preferred_element_type=jnp.float32)
        allowed = lane >= begin - at * period
        if diagonal:
            allowed = allowed & (lane <= q_index - at * period)
        weights = jnp.where(allowed, jnp.exp(scores), 0.0)
        den = den + jnp.sum(weights, axis=1, keepdims=True)
        num = num + jnp.dot(weights.astype(jnp.bfloat16), values, preferred_element_type=jnp.float32)
        return num, den

    carry = (jnp.zeros((size, HD), jnp.float32), jnp.zeros((size, 1), jnp.float32))
    carry = lax.fori_loop(0, stripe, lambda at, c: tile(at, c, False), carry)
    num, den = tile(stripe, carry, True)
    o_ref[...] = (num / den).astype(jnp.bfloat16)


def attend(meta, queries, kv, docs, stripes):
    rows, head_width = queries.shape
    plane = kv.shape[0]
    size = rows // stripes
    heads = head_width // HD
    kv = kv.reshape(plane, 2, stripes, size, head_width)
    return pl.pallas_call(
        functools.partial(attend_kernel, docs),
        grid_spec=pltpu.PrefetchScalarGridSpec(
            num_scalar_prefetch=1,
            grid=(heads, stripes),
            in_specs=[
                pl.BlockSpec((size, HD), lambda h, k, m: (k, h)),
                pl.BlockSpec((plane, None, stripes, size, HD), lambda h, k, m: (0, 0, 0, 0, h)),
                pl.BlockSpec((plane, None, stripes, size, HD), lambda h, k, m: (0, 1, 0, 0, h)),
            ],
            out_specs=pl.BlockSpec((size, HD), lambda h, k, m: (k, h)),
        ),
        out_shape=jax.ShapeDtypeStruct((rows, head_width), jnp.bfloat16),
        compiler_params=pltpu.CompilerParams(vmem_limit_bytes=VMEM_LIMIT),
        name="attend",
    )(meta, queries, kv, kv)


def output_kernel(c_ref, w_ref, o_ref):
    o_ref[0] = jnp.dot(c_ref[...], w_ref[...], preferred_element_type=jnp.float32).astype(jnp.bfloat16)


def output_terms(context, out_weight, shards):
    rows, head_width = context.shape
    width = out_weight.shape[1] // shards
    return pl.pallas_call(
        output_kernel,
        grid=(shards,),
        out_shape=jax.ShapeDtypeStruct((shards, rows, width), jnp.bfloat16),
        in_specs=[
            pl.BlockSpec((rows, head_width), lambda z: (0, 0)),
            pl.BlockSpec((head_width, width), lambda z: (0, z)),
        ],
        out_specs=pl.BlockSpec((1, rows, width), lambda z: (z, 0, 0)),
        compiler_params=pltpu.CompilerParams(vmem_limit_bytes=VMEM_LIMIT),
        name="output_terms",
    )(context, out_weight)


def per_device(hidden, depth, qkv_weight, out_weight):
    tokens = hidden[0]
    local_len = tokens.shape[0]
    docs = lax.axis_size("dp")
    ctx_count = lax.axis_size("ctx")
    shards = lax.axis_size("tensor")
    plane = docs * ctx_count
    me = lax.axis_index("dp") * ctx_count + lax.axis_index("ctx")
    size = CAP // plane
    stripes = ACT_DEV // size

    active = depth[0] >= RECURSION
    ones = active.astype(jnp.int32)
    counts = lax.all_gather(jnp.sum(ones)[None], PLANE, axis=0, tiled=True)
    ends = jnp.cumsum(counts)
    starts = ends - counts
    rank = jnp.cumsum(ones) - 1
    slot = jnp.where(active, lax.rem(starts[me] + rank, CAP), -1)
    onehot = (jnp.arange(CAP, dtype=jnp.int32)[:, None] == slot[None, :]).astype(jnp.bfloat16)
    dealt = jnp.dot(onehot, tokens, preferred_element_type=jnp.float32).astype(jnp.bfloat16)
    received = lax.all_to_all(dealt.reshape(plane, size, -1), PLANE, 0, 0)

    index = (
        jnp.arange(stripes, dtype=jnp.int32)[:, None] * CAP
        + me * size
        + jnp.arange(size, dtype=jnp.int32)[None, :]
    )
    owned = (index[None] >= starts[:, None, None]) & (index[None] < ends[:, None, None])
    zero = jnp.zeros((), jnp.bfloat16)
    packed = jnp.where(owned[0][:, :, None], received[0][None], zero)
    for b in range(1, plane):
        packed = jnp.where(owned[b][:, :, None], received[b][None], packed)
    packed = packed.reshape(ACT_DEV, -1)

    rows_all = lax.all_gather(packed, "tensor", axis=0)
    weight = jnp.transpose(qkv_weight, (1, 0, 2))
    projected = project(rows_all, weight)
    kv = lax.all_gather(projected[1:], PLANE, axis=0)
    meta = jnp.concatenate([starts[::ctx_count], me[None]]).astype(jnp.int32)
    context = attend(meta, projected[0], kv, docs, stripes)
    terms = output_terms(context, out_weight, shards)
    rows_back = lax.psum_scatter(terms, "tensor", scatter_dimension=0)

    rows_back = rows_back.reshape(stripes, size, -1)
    returned = jnp.where(owned[:, 0][:, :, None], rows_back[0][None], zero)
    for k in range(1, stripes):
        returned = jnp.where(owned[:, k][:, :, None], rows_back[k][None], returned)
    landed = lax.all_to_all(returned, PLANE, 0, 0).reshape(CAP, -1)
    spread = (slot[:, None] == jnp.arange(CAP, dtype=jnp.int32)[None, :]).astype(jnp.bfloat16)
    update = jnp.dot(spread, landed, preferred_element_type=jnp.float32).astype(jnp.bfloat16)
    return update[None]


def solution(mesh):
    placed = (P("dp", "ctx", "tensor"), P("dp", "ctx"), P(None, None, "tensor"), P("tensor", None))
    return jax.shard_map(
        per_device, mesh=mesh, in_specs=placed, out_specs=P("dp", "ctx", "tensor"), check_vma=False
    )
```

```python
import functools

import jax
import jax.numpy as jnp
from jax import lax
from jax.experimental import pallas as pl
from jax.experimental.pallas import tpu as pltpu
from jax.sharding import PartitionSpec as P

HD = 128
RECURSION = 3
CAP = 1024
ACT_DEV = 512

score_scale = 0.25
norm_epsilon = 1e-05
head_epsilon = 1e-06
VMEM_LIMIT = 60 * 1024 * 1024
PLANE = ("dp", "ctx")


def project_kernel(x_ref, w_ref, q_ref, kv_ref, normed):
    part = pl.program_id(0)
    shards, rows, width = x_ref.shape

    @pl.when(part == 0)
    def _():
        total = jnp.zeros((rows, 1), jnp.float32)
        for z in range(shards):
            wide = x_ref[z].astype(jnp.float32)
            total = total + jnp.sum(wide * wide, axis=1, keepdims=True)
        factor = lax.rsqrt(total / (shards * width) + norm_epsilon)
        for z in range(shards):
            normed[z] = (x_ref[z].astype(jnp.float32) * factor).astype(jnp.bfloat16)

    acc = jnp.dot(normed[0], w_ref[0, :width], preferred_element_type=jnp.float32)
    for z in range(1, shards):
        acc = acc + jnp.dot(normed[z], w_ref[0, z * width : (z + 1) * width], preferred_element_type=jnp.float32)
    heads = acc.shape[1] // HD

    def head_normed(scale):
        parts = []
        for h in range(heads):
            head = acc[:, h * HD : (h + 1) * HD]
            factor = lax.rsqrt(jnp.mean(head * head, axis=1, keepdims=True) + head_epsilon) * scale
            parts.append((head * factor).astype(jnp.bfloat16))
        return parts

    @pl.when(part == 0)
    def _():
        for h, value in enumerate(head_normed(score_scale)):
            q_ref[:, h * HD : (h + 1) * HD] = value

    @pl.when(part == 1)
    def _():
        for h, value in enumerate(head_normed(1.0)):
            kv_ref[0, :, h * HD : (h + 1) * HD] = value

    @pl.when(part == 2)
    def _():
        kv_ref[0] = acc.astype(jnp.bfloat16)


def project(rows_all, weight):
    shards, rows, width = rows_all.shape
    head_width = weight.shape[2]
    flops = 2 * rows * shards * width * 3 * head_width
    return pl.pallas_call(
        project_kernel,
        grid=(3,),
        out_shape=[
            jax.ShapeDtypeStruct((rows, head_width), jnp.bfloat16),
            jax.ShapeDtypeStruct((2, rows, head_width), jnp.bfloat16),
        ],
        in_specs=[
            pl.BlockSpec((shards, rows, width), lambda p: (0, 0, 0)),
            pl.BlockSpec((1, shards * width, head_width), lambda p: (p, 0, 0)),
        ],
        out_specs=[
            pl.BlockSpec((rows, head_width), lambda p: (0, 0)),
            pl.BlockSpec((1, rows, head_width), lambda p: (jnp.maximum(p - 1, 0), 0, 0)),
        ],
        scratch_shapes=[pltpu.VMEM((shards, rows, width), jnp.bfloat16)],
        compiler_params=pltpu.CompilerParams(vmem_limit_bytes=VMEM_LIMIT),
        cost_estimate=pl.CostEstimate(flops=flops, bytes_accessed=2 * weight.size, transcendentals=0),
        name="project",
    )(rows_all, weight)


def gather_kernel(pieces, kv_ref, out_ref, send_sem, recv_sem, local_sem):
    x, place = lax.axis_index("dp"), lax.axis_index("ctx")
    y, core = place // 2, lax.rem(place, 2)
    rows = kv_ref.shape[1] // pieces

    def block(flip_x, flip_y, flip_core):
        return (x ^ flip_x) * 4 + (y ^ flip_y) * 2 + (core ^ flip_core)

    def device(flip_x, flip_y, flip_core):
        return {"dp": x ^ flip_x, "ctx": (y ^ flip_y) * 2 + (core ^ flip_core)}

    sibling, across_x, across_y = device(0, 0, 1), device(1, 0, 0), device(0, 1, 0)
    barrier = pltpu.get_barrier_semaphore()
    for target in (sibling, across_x, across_y):
        pl.semaphore_signal(barrier, inc=1, device_id=target, device_id_type=pl.DeviceIdType.MESH)
    pl.semaphore_wait(barrier, 3)

    me = block(0, 0, 0)
    local = pltpu.make_async_copy(kv_ref, out_ref.at[me], local_sem)
    local.start()
    sends = []

    def send(origin, route, piece, target, own=False):
        window = pl.ds(piece * rows, rows)
        copy = pltpu.make_async_remote_copy(
            src_ref=kv_ref.at[:, window] if own else out_ref.at[origin, :, window],
            dst_ref=out_ref.at[origin, :, window],
            send_sem=send_sem.at[route, piece],
            recv_sem=recv_sem.at[route, piece],
            device_id=target,
            device_id_type=pl.DeviceIdType.MESH,
        )
        copy.start()
        sends.append(copy)

    def arrive(origin, route, piece):
        window = pl.ds(piece * rows, rows)
        pltpu.make_async_remote_copy(
            src_ref=out_ref.at[origin, :, window],
            dst_ref=out_ref.at[origin, :, window],
            send_sem=send_sem.at[route, piece],
            recv_sem=recv_sem.at[route, piece],
            device_id=sibling,
            device_id_type=pl.DeviceIdType.MESH,
        ).wait_recv()

    for piece in range(pieces):
        send(me, 1, piece, across_x, True)
        send(me, 2, piece, across_y, True)
        send(me, 0, piece, sibling, True)
    first = core == 0
    onward = jnp.where(first, block(0, 1, 0), block(1, 0, 0))
    onward_device = {
        "dp": jnp.where(first, x ^ 1, x),
        "ctx": jnp.where(first, place, (y ^ 1) * 2 + core),
    }
    for piece in range(pieces):
        arrive(block(1, 0, 0), 1, piece)
        arrive(block(0, 1, 0), 2, piece)
        send(onward, 3, piece, onward_device)
        send(block(1, 0, 0), 4, piece, sibling)
        send(block(0, 1, 0), 5, piece, sibling)
    for piece in range(pieces):
        arrive(block(1, 1, 0), 3, piece)
        send(block(1, 1, 0), 6, piece, sibling)
    for piece in range(pieces):
        arrive(block(0, 0, 1), 0, piece)
        arrive(block(1, 0, 1), 4, piece)
        arrive(block(0, 1, 1), 5, piece)
        arrive(block(1, 1, 1), 6, piece)
    for copy in sends:
        copy.wait_send()
    local.wait()


def gather_plane(kv, call):
    docs, ctx_count = lax.axis_size("dp"), lax.axis_size("ctx")
    if (docs, ctx_count) != (2, 4):
        return lax.all_gather(kv, PLANE, axis=0)
    pieces = 4
    plane = docs * ctx_count
    return pl.pallas_call(
        functools.partial(gather_kernel, pieces),
        out_shape=jax.ShapeDtypeStruct((plane,) + kv.shape, kv.dtype),
        in_specs=[pl.BlockSpec(memory_space=pltpu.VMEM)],
        out_specs=pl.BlockSpec(memory_space=pl.ANY),
        scratch_shapes=[
            pltpu.SemaphoreType.DMA((7, pieces)),
            pltpu.SemaphoreType.DMA((7, pieces)),
            pltpu.SemaphoreType.DMA,
        ],
        compiler_params=pltpu.CompilerParams(collective_id=call, has_side_effects=True),
        cost_estimate=pl.CostEstimate(flops=0, bytes_accessed=60_000_000, transcendentals=0),
        name="gather_plane",
    )(kv)


def attend_kernel(docs, base, meta_ref, q_ref, *refs):
    o_ref = refs[-1]
    pairs = [(refs[i], refs[i + 1]) for i in range(0, len(refs) - 1, 2)]
    plane, stripes, size, _ = refs[0].shape
    period = plane * size
    rows = stripes * size
    me = meta_ref[docs]
    row = lax.broadcasted_iota(jnp.int32, (rows, 1), 0)
    q_index = (base + row // size) * period + me * size + lax.rem(row, size)
    begin = jnp.zeros((rows, 1), jnp.int32)
    for d in range(docs):
        begin = jnp.where(q_index >= meta_ref[d], meta_ref[d], begin)
    lane = lax.broadcasted_iota(jnp.int32, (1, period), 1)
    query = q_ref[...]
    num = jnp.zeros((rows, HD), jnp.float32)
    den = jnp.zeros((rows, 1), jnp.float32)
    at = 0
    for k_ref, v_ref in pairs:
        for k in range(stripes):
            keys = k_ref[:, k].reshape(period, HD)
            values = v_ref[:, k].reshape(period, HD)
            scores = lax.dot_general(query, keys, (((1,), (1,)), ((), ())), preferred_element_type=jnp.float32)
            allowed = lane >= begin - at * period
            if at >= base:
                allowed = allowed & (lane <= q_index - at * period)
            weights = jnp.where(allowed, jnp.exp(scores), 0.0)
            den = den + jnp.sum(weights, axis=1, keepdims=True)
            num = num + jnp.dot(weights.astype(jnp.bfloat16), values, preferred_element_type=jnp.float32)
            at += 1
    o_ref[...] = (num / den).astype(jnp.bfloat16)


def attend(meta, queries, kvs, docs, stripes):
    rows, head_width = queries.shape
    plane = kvs[0].shape[0]
    size = rows // stripes
    heads = head_width // HD
    operands, specs = [], []
    for kv in kvs:
        kv = kv.reshape(plane, 2, stripes, size, head_width)
        for which in range(2):
            operands.append(kv)
            specs.append(
                pl.BlockSpec((plane, None, stripes, size, HD), lambda h, m, which=which: (0, which, 0, 0, h))
            )
    pairs = rows * plane * rows * len(kvs)
    return pl.pallas_call(
        functools.partial(attend_kernel, docs, (len(kvs) - 1) * stripes),
        grid_spec=pltpu.PrefetchScalarGridSpec(
            num_scalar_prefetch=1,
            grid=(heads,),
            in_specs=[pl.BlockSpec((rows, HD), lambda h, m: (0, h))] + specs,
            out_specs=pl.BlockSpec((rows, HD), lambda h, m: (0, h)),
        ),
        out_shape=jax.ShapeDtypeStruct((rows, head_width), jnp.bfloat16),
        compiler_params=pltpu.CompilerParams(vmem_limit_bytes=VMEM_LIMIT),
        cost_estimate=pl.CostEstimate(
            flops=4 * pairs * head_width, bytes_accessed=4 * kvs[0].size, transcendentals=pairs * heads
        ),
        name="attend",
    )(meta, queries, *operands)


def output_kernel(c_ref, w_ref, o_ref):
    o_ref[0] = jnp.dot(c_ref[...], w_ref[...], preferred_element_type=jnp.float32).astype(jnp.bfloat16)


def output_terms(context, out_weight, shards):
    rows, head_width = context.shape
    width = out_weight.shape[1] // shards
    return pl.pallas_call(
        output_kernel,
        grid=(shards,),
        out_shape=jax.ShapeDtypeStruct((shards, rows, width), jnp.bfloat16),
        in_specs=[
            pl.BlockSpec((rows, head_width), lambda z: (0, 0)),
            pl.BlockSpec((head_width, width), lambda z: (0, z)),
        ],
        out_specs=pl.BlockSpec((1, rows, width), lambda z: (z, 0, 0)),
        compiler_params=pltpu.CompilerParams(vmem_limit_bytes=VMEM_LIMIT),
        name="output_terms",
    )(context, out_weight)


def per_device(hidden, depth, qkv_weight, out_weight):
    tokens = hidden[0]
    local_len = tokens.shape[0]
    docs = lax.axis_size("dp")
    ctx_count = lax.axis_size("ctx")
    shards = lax.axis_size("tensor")
    plane = docs * ctx_count
    me = lax.axis_index("dp") * ctx_count + lax.axis_index("ctx")
    size = CAP // plane
    stripes = ACT_DEV // size

    active = depth[0] >= RECURSION
    ones = active.astype(jnp.int32)
    counts = lax.all_gather(jnp.sum(ones)[None], PLANE, axis=0, tiled=True)
    ends = jnp.cumsum(counts)
    starts = ends - counts
    rank = jnp.cumsum(ones) - 1
    slot = jnp.where(active, lax.rem(starts[me] + rank, CAP), -1)
    onehot = (jnp.arange(CAP, dtype=jnp.int32)[:, None] == slot[None, :]).astype(jnp.bfloat16)
    dealt = jnp.dot(onehot, tokens, preferred_element_type=jnp.float32).astype(jnp.bfloat16)
    received = lax.all_to_all(dealt.reshape(plane, size, -1), PLANE, 0, 0)

    index = (
        jnp.arange(stripes, dtype=jnp.int32)[:, None] * CAP
        + me * size
        + jnp.arange(size, dtype=jnp.int32)[None, :]
    )
    owned = (index[None] >= starts[:, None, None]) & (index[None] < ends[:, None, None])
    zero = jnp.zeros((), jnp.bfloat16)
    packed = jnp.where(owned[0][:, :, None], received[0][None], zero)
    for b in range(1, plane):
        packed = jnp.where(owned[b][:, :, None], received[b][None], packed)
    packed = packed.reshape(ACT_DEV, -1)

    chunks = 2
    chunk_stripes = stripes // chunks
    chunk_rows = ACT_DEV // chunks
    weight = jnp.transpose(qkv_weight, (1, 0, 2))
    meta = jnp.concatenate([starts[::ctx_count], me[None]]).astype(jnp.int32)
    rows_all = [
        lax.all_gather(packed[c * chunk_rows : (c + 1) * chunk_rows], "tensor", axis=0) for c in range(chunks)
    ]
    kvs, backs = [], []
    for c in range(chunks):
        queries, kv = project(rows_all[c], weight)
        kvs.append(gather_plane(kv, c))
        context = attend(meta, queries, kvs, docs, chunk_stripes)
        terms = output_terms(context, out_weight, shards)
        backs.append(lax.psum_scatter(terms, "tensor", scatter_dimension=0))
    rows_back = jnp.concatenate(backs, axis=0)

    rows_back = rows_back.reshape(stripes, size, -1)
    returned = jnp.where(owned[:, 0][:, :, None], rows_back[0][None], zero)
    for k in range(1, stripes):
        returned = jnp.where(owned[:, k][:, :, None], rows_back[k][None], returned)
    landed = lax.all_to_all(returned, PLANE, 0, 0).reshape(CAP, -1)
    spread = (slot[:, None] == jnp.arange(CAP, dtype=jnp.int32)[None, :]).astype(jnp.bfloat16)
    update = jnp.dot(spread, landed, preferred_element_type=jnp.float32).astype(jnp.bfloat16)
    return update[None]


def solution(mesh):
    placed = (P("dp", "ctx", "tensor"), P("dp", "ctx"), P(None, None, "tensor"), P("tensor", None))
    return jax.shard_map(
        per_device, mesh=mesh, in_specs=placed, out_specs=P("dp", "ctx", "tensor"), check_vma=False
    )
```

```python
import functools

import jax
import jax.numpy as jnp
from jax import lax
from jax.experimental import pallas as pl
from jax.experimental.pallas import tpu as pltpu
from jax.sharding import PartitionSpec as P

HD = 128
RECURSION = 3
CAP = 1024
ACT_DEV = 512

score_scale = 0.25
norm_epsilon = 1e-05
head_epsilon = 1e-06
VMEM_LIMIT = 60 * 1024 * 1024
PLANE = ("dp", "ctx")


def project_kernel(x_ref, w_ref, q_ref, kv_ref, normed):
    part = pl.program_id(0)
    shards, rows, width = x_ref.shape

    @pl.when(part == 0)
    def _():
        total = jnp.zeros((rows, 1), jnp.float32)
        for z in range(shards):
            wide = x_ref[z].astype(jnp.float32)
            total = total + jnp.sum(wide * wide, axis=1, keepdims=True)
        factor = lax.rsqrt(total / (shards * width) + norm_epsilon)
        for z in range(shards):
            normed[z] = (x_ref[z].astype(jnp.float32) * factor).astype(jnp.bfloat16)

    acc = jnp.dot(normed[0], w_ref[0, :width], preferred_element_type=jnp.float32)
    for z in range(1, shards):
        acc = acc + jnp.dot(normed[z], w_ref[0, z * width : (z + 1) * width], preferred_element_type=jnp.float32)
    heads = acc.shape[1] // HD

    def head_normed(scale):
        parts = []
        for h in range(heads):
            head = acc[:, h * HD : (h + 1) * HD]
            factor = lax.rsqrt(jnp.mean(head * head, axis=1, keepdims=True) + head_epsilon) * scale
            parts.append((head * factor).astype(jnp.bfloat16))
        return parts

    @pl.when(part == 0)
    def _():
        for h, value in enumerate(head_normed(score_scale)):
            q_ref[:, h * HD : (h + 1) * HD] = value

    @pl.when(part == 1)
    def _():
        for h, value in enumerate(head_normed(1.0)):
            kv_ref[0, :, h * HD : (h + 1) * HD] = value

    @pl.when(part == 2)
    def _():
        kv_ref[0] = acc.astype(jnp.bfloat16)


def project(rows_all, weight):
    shards, rows, width = rows_all.shape
    head_width = weight.shape[2]
    flops = 2 * rows * shards * width * 3 * head_width
    return pl.pallas_call(
        project_kernel,
        grid=(3,),
        out_shape=[
            jax.ShapeDtypeStruct((rows, head_width), jnp.bfloat16),
            jax.ShapeDtypeStruct((2, rows, head_width), jnp.bfloat16),
        ],
        in_specs=[
            pl.BlockSpec((shards, rows, width), lambda p: (0, 0, 0)),
            pl.BlockSpec((1, shards * width, head_width), lambda p: (p, 0, 0)),
        ],
        out_specs=[
            pl.BlockSpec((rows, head_width), lambda p: (0, 0)),
            pl.BlockSpec((1, rows, head_width), lambda p: (jnp.maximum(p - 1, 0), 0, 0)),
        ],
        scratch_shapes=[pltpu.VMEM((shards, rows, width), jnp.bfloat16)],
        compiler_params=pltpu.CompilerParams(vmem_limit_bytes=VMEM_LIMIT),
        cost_estimate=pl.CostEstimate(flops=flops, bytes_accessed=2 * weight.size, transcendentals=0),
        name="project",
    )(rows_all, weight)


def gather_plane(kv):
    docs, ctx_count = lax.axis_size("dp"), lax.axis_size("ctx")
    if (docs, ctx_count) != (2, 4):
        return [(lax.all_gather(kv, PLANE, axis=0), jnp.zeros((), jnp.int32))]
    me = lax.axis_index("dp") * ctx_count + lax.axis_index("ctx")
    plane = docs * ctx_count
    x_flip, y_flip, core_flip = ctx_count, 2, 1

    def move(value, flip):
        return lax.ppermute(value, PLANE, [(i, i ^ flip) for i in range(plane)])

    from_x = move(kv, x_flip)
    from_y = move(kv, y_flip)
    even = lax.rem(me, 2) == 0
    onward = jnp.where(even, from_y, from_x)
    from_diagonal = lax.ppermute(
        onward, PLANE, [(i, i ^ (y_flip if i % 2 else x_flip)) for i in range(plane)]
    )
    blocks = [(kv, 0), (move(kv, core_flip), core_flip)]
    for value, flip in ((from_x, x_flip), (from_y, y_flip), (from_diagonal, x_flip ^ y_flip)):
        blocks.append((value, flip))
        blocks.append((move(value, core_flip), flip ^ core_flip))
    return [(value[None], me ^ flip) for value, flip in blocks]


def attend_kernel(docs, base, stripes, period, meta_ref, q_ref, *refs):
    o_ref = refs[-1]
    rows = q_ref.shape[0]
    size = rows // stripes
    me = meta_ref[docs]

    def index_of(at, place, first):
        return (first + at // size) * period + place * size + lax.rem(at, size)

    q_index = index_of(lax.broadcasted_iota(jnp.int32, (rows, 1), 0), me, base)
    lane_at = lax.broadcasted_iota(jnp.int32, (1, rows), 1)
    begin = jnp.zeros((rows, 1), jnp.int32)
    for d in range(docs):
        begin = jnp.where(q_index >= meta_ref[d], meta_ref[d], begin)
    query = q_ref[...]
    num = jnp.zeros((rows, HD), jnp.float32)
    den = jnp.zeros((rows, 1), jnp.float32)
    arrays = (len(refs) - 1) // 2
    per_chunk = arrays // (base // stripes + 1)
    for i in range(arrays):
        k_ref, v_ref = refs[2 * i], refs[2 * i + 1]
        first = i // per_chunk * stripes
        for piece in range(k_ref.shape[0]):
            k_index = index_of(lane_at, meta_ref[docs + 1 + i] + piece, first)
            scores = lax.dot_general(
                query, k_ref[piece], (((1,), (1,)), ((), ())), preferred_element_type=jnp.float32
            )
            allowed = k_index >= begin
            if first == base:
                allowed = allowed & (k_index <= q_index)
            weights = jnp.where(allowed, jnp.exp(scores), 0.0)
            den = den + jnp.sum(weights, axis=1, keepdims=True)
            num = num + jnp.dot(weights.astype(jnp.bfloat16), v_ref[piece], preferred_element_type=jnp.float32)
    o_ref[...] = (num / den).astype(jnp.bfloat16)


def attend(meta, queries, kvs, chunk, docs, stripes, period):
    rows, head_width = queries.shape
    heads = head_width // HD
    operands, specs = [], []
    for kv, _ in kvs:
        for which in range(2):
            operands.append(kv)
            specs.append(
                pl.BlockSpec((kv.shape[0], None, rows, HD), lambda h, m, which=which: (0, which, 0, h))
            )
    meta = jnp.concatenate([meta, jnp.stack([place for _, place in kvs]).astype(jnp.int32)])
    pairs = rows * rows * sum(kv.shape[0] for kv, _ in kvs)
    return pl.pallas_call(
        functools.partial(attend_kernel, docs, chunk * stripes, stripes, period),
        grid_spec=pltpu.PrefetchScalarGridSpec(
            num_scalar_prefetch=1,
            grid=(heads,),
            in_specs=[pl.BlockSpec((rows, HD), lambda h, m: (0, h))] + specs,
            out_specs=pl.BlockSpec((rows, HD), lambda h, m: (0, h)),
        ),
        out_shape=jax.ShapeDtypeStruct((rows, head_width), jnp.bfloat16),
        compiler_params=pltpu.CompilerParams(vmem_limit_bytes=VMEM_LIMIT),
        cost_estimate=pl.CostEstimate(
            flops=4 * pairs * head_width, bytes_accessed=2 * queries.size, transcendentals=pairs * heads
        ),
        name="attend",
    )(meta, queries, *operands)


def output_kernel(c_ref, w_ref, o_ref):
    o_ref[0] = jnp.dot(c_ref[...], w_ref[...], preferred_element_type=jnp.float32).astype(jnp.bfloat16)


def output_terms(context, out_weight, shards):
    rows, head_width = context.shape
    width = out_weight.shape[1] // shards
    return pl.pallas_call(
        output_kernel,
        grid=(shards,),
        out_shape=jax.ShapeDtypeStruct((shards, rows, width), jnp.bfloat16),
        in_specs=[
            pl.BlockSpec((rows, head_width), lambda z: (0, 0)),
            pl.BlockSpec((head_width, width), lambda z: (0, z)),
        ],
        out_specs=pl.BlockSpec((1, rows, width), lambda z: (z, 0, 0)),
        compiler_params=pltpu.CompilerParams(vmem_limit_bytes=VMEM_LIMIT),
        name="output_terms",
    )(context, out_weight)


def per_device(hidden, depth, qkv_weight, out_weight):
    tokens = hidden[0]
    local_len = tokens.shape[0]
    docs = lax.axis_size("dp")
    ctx_count = lax.axis_size("ctx")
    shards = lax.axis_size("tensor")
    plane = docs * ctx_count
    me = lax.axis_index("dp") * ctx_count + lax.axis_index("ctx")
    size = CAP // plane
    stripes = ACT_DEV // size

    active = depth[0] >= RECURSION
    ones = active.astype(jnp.int32)
    counts = lax.all_gather(jnp.sum(ones)[None], PLANE, axis=0, tiled=True)
    ends = jnp.cumsum(counts)
    starts = ends - counts
    rank = jnp.cumsum(ones) - 1
    slot = jnp.where(active, lax.rem(starts[me] + rank, CAP), -1)
    onehot = (jnp.arange(CAP, dtype=jnp.int32)[:, None] == slot[None, :]).astype(jnp.bfloat16)
    dealt = jnp.dot(onehot, tokens, preferred_element_type=jnp.float32).astype(jnp.bfloat16)
    received = lax.all_to_all(dealt.reshape(plane, size, -1), PLANE, 0, 0)

    index = (
        jnp.arange(stripes, dtype=jnp.int32)[:, None] * CAP
        + me * size
        + jnp.arange(size, dtype=jnp.int32)[None, :]
    )
    owned = (index[None] >= starts[:, None, None]) & (index[None] < ends[:, None, None])
    zero = jnp.zeros((), jnp.bfloat16)
    packed = jnp.where(owned[0][:, :, None], received[0][None], zero)
    for b in range(1, plane):
        packed = jnp.where(owned[b][:, :, None], received[b][None], packed)
    packed = packed.reshape(ACT_DEV, -1)

    chunks = 4
    chunk_stripes = stripes // chunks
    chunk_rows = ACT_DEV // chunks
    weight = jnp.transpose(qkv_weight, (1, 0, 2))
    meta = jnp.concatenate([starts[::ctx_count], me[None]]).astype(jnp.int32)
    rows_all = [
        lax.all_gather(packed[c * chunk_rows : (c + 1) * chunk_rows], "tensor", axis=0) for c in range(chunks)
    ]
    kvs, backs = [], []
    for c in range(chunks):
        queries, kv = project(rows_all[c], weight)
        kvs = kvs + gather_plane(kv)
        context = attend(meta, queries, kvs, c, docs, chunk_stripes, CAP)
        terms = output_terms(context, out_weight, shards)
        backs.append(lax.psum_scatter(terms, "tensor", scatter_dimension=0))
    rows_back = jnp.concatenate(backs, axis=0)

    rows_back = rows_back.reshape(stripes, size, -1)
    returned = jnp.where(owned[:, 0][:, :, None], rows_back[0][None], zero)
    for k in range(1, stripes):
        returned = jnp.where(owned[:, k][:, :, None], rows_back[k][None], returned)
    landed = lax.all_to_all(returned, PLANE, 0, 0).reshape(CAP, -1)
    spread = (slot[:, None] == jnp.arange(CAP, dtype=jnp.int32)[None, :]).astype(jnp.bfloat16)
    update = jnp.dot(spread, landed, preferred_element_type=jnp.float32).astype(jnp.bfloat16)
    return update[None]


def solution(mesh):
    placed = (P("dp", "ctx", "tensor"), P("dp", "ctx"), P(None, None, "tensor"), P("tensor", None))
    return jax.shard_map(
        per_device, mesh=mesh, in_specs=placed, out_specs=P("dp", "ctx", "tensor"), check_vma=False
    )
```

```python
import functools

import jax
import jax.numpy as jnp
from jax import lax
from jax.experimental import pallas as pl
from jax.experimental.pallas import tpu as pltpu
from jax.sharding import PartitionSpec as P

HD = 128
RECURSION = 3
CAP = 1024
ACT_DEV = 512

score_scale = 0.25
norm_epsilon = 1e-05
head_epsilon = 1e-06
VMEM_LIMIT = 60 * 1024 * 1024
PLANE = ("dp", "ctx")
TILE = 256
ALIGN = 16
WINDOW = TILE + ALIGN


def selection(relative_ref):
    at = lax.broadcasted_iota(jnp.int32, (WINDOW, TILE), 0)
    return jnp.where(at == relative_ref[0], 1.0, 0.0).astype(jnp.bfloat16)


def window_of(base_ref, tile):
    return pl.ds(pl.multiple_of(base_ref[tile] // ALIGN * ALIGN, ALIGN), WINDOW)


def deal_kernel(base_ref, relative_ref, token_ref, o_ref, total):
    tile = pl.program_id(0)

    @pl.when(tile == 0)
    def _():
        total[...] = jnp.zeros_like(total)

    window = window_of(base_ref, tile)
    total[window] += jnp.dot(selection(relative_ref), token_ref[...], preferred_element_type=jnp.float32)

    @pl.when(tile == pl.num_programs(0) - 1)
    def _():
        o_ref[:WINDOW] = (total[:WINDOW] + total[CAP:]).astype(jnp.bfloat16)
        o_ref[WINDOW:] = total[WINDOW:CAP].astype(jnp.bfloat16)


def deal(base, relative, tokens):
    local_len, width = tokens.shape
    return pl.pallas_call(
        deal_kernel,
        grid_spec=pltpu.PrefetchScalarGridSpec(
            num_scalar_prefetch=1,
            grid=(local_len // TILE,),
            in_specs=[
                pl.BlockSpec((1, 1, TILE), lambda t, m: (t, 0, 0)),
                pl.BlockSpec((TILE, width), lambda t, m: (t, 0)),
            ],
            out_specs=pl.BlockSpec((CAP, width), lambda t, m: (0, 0)),
            scratch_shapes=[pltpu.VMEM((CAP + WINDOW, width), jnp.float32)],
        ),
        out_shape=jax.ShapeDtypeStruct((CAP, width), jnp.bfloat16),
        compiler_params=pltpu.CompilerParams(vmem_limit_bytes=VMEM_LIMIT),
        name="deal",
    )(base, relative, tokens)


def spread_kernel(base_ref, relative_ref, row_ref, o_ref, wrapped):
    tile = pl.program_id(0)

    @pl.when(tile == 0)
    def _():
        wrapped[:CAP] = row_ref[...]
        wrapped[CAP:] = row_ref[:WINDOW]

    rows = wrapped[window_of(base_ref, tile)]
    o_ref[...] = lax.dot_general(
        selection(relative_ref), rows, (((0,), (0,)), ((), ())), preferred_element_type=jnp.float32
    ).astype(jnp.bfloat16)


def spread(base, relative, rows):
    tiles = relative.shape[0]
    width = rows.shape[1]
    return pl.pallas_call(
        spread_kernel,
        grid_spec=pltpu.PrefetchScalarGridSpec(
            num_scalar_prefetch=1,
            grid=(tiles,),
            in_specs=[
                pl.BlockSpec((1, 1, TILE), lambda t, m: (t, 0, 0)),
                pl.BlockSpec((CAP, width), lambda t, m: (0, 0)),
            ],
            out_specs=pl.BlockSpec((TILE, width), lambda t, m: (t, 0)),
            scratch_shapes=[pltpu.VMEM((CAP + WINDOW, width), jnp.bfloat16)],
        ),
        out_shape=jax.ShapeDtypeStruct((tiles * TILE, width), jnp.bfloat16),
        compiler_params=pltpu.CompilerParams(vmem_limit_bytes=VMEM_LIMIT),
        name="spread",
    )(base, relative, rows)


def project_kernel(x_ref, w_ref, q_ref, kv_ref, normed):
    part = pl.program_id(0)
    shards, rows, width = x_ref.shape

    @pl.when(part == 0)
    def _():
        total = jnp.zeros((rows, 1), jnp.float32)
        for z in range(shards):
            wide = x_ref[z].astype(jnp.float32)
            total = total + jnp.sum(wide * wide, axis=1, keepdims=True)
        factor = lax.rsqrt(total / (shards * width) + norm_epsilon)
        for z in range(shards):
            normed[z] = (x_ref[z].astype(jnp.float32) * factor).astype(jnp.bfloat16)

    acc = jnp.dot(normed[0], w_ref[0, :width], preferred_element_type=jnp.float32)
    for z in range(1, shards):
        acc = acc + jnp.dot(normed[z], w_ref[0, z * width : (z + 1) * width], preferred_element_type=jnp.float32)
    heads = acc.shape[1] // HD

    def head_normed(scale):
        parts = []
        for h in range(heads):
            head = acc[:, h * HD : (h + 1) * HD]
            factor = lax.rsqrt(jnp.mean(head * head, axis=1, keepdims=True) + head_epsilon) * scale
            parts.append((head * factor).astype(jnp.bfloat16))
        return parts

    @pl.when(part == 0)
    def _():
        for h, value in enumerate(head_normed(score_scale)):
            q_ref[:, h * HD : (h + 1) * HD] = value

    @pl.when(part == 1)
    def _():
        for h, value in enumerate(head_normed(1.0)):
            kv_ref[0, :, h * HD : (h + 1) * HD] = value

    @pl.when(part == 2)
    def _():
        kv_ref[0] = acc.astype(jnp.bfloat16)


def project(rows_all, weight):
    shards, rows, width = rows_all.shape
    head_width = weight.shape[2]
    flops = 2 * rows * shards * width * 3 * head_width
    return pl.pallas_call(
        project_kernel,
        grid=(3,),
        out_shape=[
            jax.ShapeDtypeStruct((rows, head_width), jnp.bfloat16),
            jax.ShapeDtypeStruct((2, rows, head_width), jnp.bfloat16),
        ],
        in_specs=[
            pl.BlockSpec((shards, rows, width), lambda p: (0, 0, 0)),
            pl.BlockSpec((1, shards * width, head_width), lambda p: (p, 0, 0)),
        ],
        out_specs=[
            pl.BlockSpec((rows, head_width), lambda p: (0, 0)),
            pl.BlockSpec((1, rows, head_width), lambda p: (jnp.maximum(p - 1, 0), 0, 0)),
        ],
        scratch_shapes=[pltpu.VMEM((shards, rows, width), jnp.bfloat16)],
        compiler_params=pltpu.CompilerParams(vmem_limit_bytes=VMEM_LIMIT),
        cost_estimate=pl.CostEstimate(flops=flops, bytes_accessed=2 * weight.size, transcendentals=0),
        name="project",
    )(rows_all, weight)


def gather_plane(kv, beside):
    docs, ctx_count = lax.axis_size("dp"), lax.axis_size("ctx")
    if (docs, ctx_count) != (2, 4):
        return [(lax.all_gather(kv, PLANE, axis=0), jnp.zeros((), jnp.int32))], beside
    me = lax.axis_index("dp") * ctx_count + lax.axis_index("ctx")
    plane = docs * ctx_count
    x_flip, y_flip, core_flip = ctx_count, 2, 1

    def move(value, flip):
        return lax.ppermute(value, PLANE, [(i, i ^ flip) for i in range(plane)])

    from_x = move(kv, x_flip)
    from_y = move(kv, y_flip)
    if beside is not None:
        from_x, from_y, beside = lax.optimization_barrier((from_x, from_y, beside))
    even = lax.rem(me, 2) == 0
    onward = jnp.where(even, from_y, from_x)
    from_diagonal = lax.ppermute(
        onward, PLANE, [(i, i ^ (y_flip if i % 2 else x_flip)) for i in range(plane)]
    )
    blocks = [(kv, 0), (move(kv, core_flip), core_flip)]
    for value, flip in ((from_x, x_flip), (from_y, y_flip), (from_diagonal, x_flip ^ y_flip)):
        blocks.append((value, flip))
        blocks.append((move(value, core_flip), flip ^ core_flip))
    return [(value[None], me ^ flip) for value, flip in blocks], beside


def attend_kernel(docs, base, stripes, period, meta_ref, q_ref, *refs):
    o_ref = refs[-1]
    rows = q_ref.shape[0]
    size = rows // stripes
    me = meta_ref[docs]

    def index_of(at, place, first):
        return (first + at // size) * period + place * size + lax.rem(at, size)

    q_index = index_of(lax.broadcasted_iota(jnp.int32, (rows, 1), 0), me, base)
    lane_at = lax.broadcasted_iota(jnp.int32, (1, rows), 1)
    begin = jnp.zeros((rows, 1), jnp.int32)
    for d in range(docs):
        begin = jnp.where(q_index >= meta_ref[d], meta_ref[d], begin)
    query = q_ref[...]
    num = jnp.zeros((rows, HD), jnp.float32)
    den = jnp.zeros((rows, 1), jnp.float32)
    arrays = (len(refs) - 1) // 2
    per_chunk = arrays // (base // stripes + 1)
    for i in range(arrays):
        k_ref, v_ref = refs[2 * i], refs[2 * i + 1]
        first = i // per_chunk * stripes
        for piece in range(k_ref.shape[0]):
            k_index = index_of(lane_at, meta_ref[docs + 1 + i] + piece, first)
            scores = lax.dot_general(
                query, k_ref[piece], (((1,), (1,)), ((), ())), preferred_element_type=jnp.float32
            )
            allowed = k_index >= begin
            if first == base:
                allowed = allowed & (k_index <= q_index)
            weights = jnp.where(allowed, jnp.exp(scores), 0.0)
            den = den + jnp.sum(weights, axis=1, keepdims=True)
            num = num + jnp.dot(weights.astype(jnp.bfloat16), v_ref[piece], preferred_element_type=jnp.float32)
    o_ref[...] = (num / den).astype(jnp.bfloat16)


def attend(meta, queries, kvs, chunk, docs, stripes, period):
    rows, head_width = queries.shape
    heads = head_width // HD
    operands, specs = [], []
    for kv, _ in kvs:
        for which in range(2):
            operands.append(kv)
            specs.append(
                pl.BlockSpec((kv.shape[0], None, rows, HD), lambda h, m, which=which: (0, which, 0, h))
            )
    meta = jnp.concatenate([meta, jnp.stack([place for _, place in kvs]).astype(jnp.int32)])
    pairs = rows * rows * sum(kv.shape[0] for kv, _ in kvs)
    return pl.pallas_call(
        functools.partial(attend_kernel, docs, chunk * stripes, stripes, period),
        grid_spec=pltpu.PrefetchScalarGridSpec(
            num_scalar_prefetch=1,
            grid=(heads,),
            in_specs=[pl.BlockSpec((rows, HD), lambda h, m: (0, h))] + specs,
            out_specs=pl.BlockSpec((rows, HD), lambda h, m: (0, h)),
        ),
        out_shape=jax.ShapeDtypeStruct((rows, head_width), jnp.bfloat16),
        compiler_params=pltpu.CompilerParams(vmem_limit_bytes=VMEM_LIMIT),
        cost_estimate=pl.CostEstimate(
            flops=4 * pairs * head_width, bytes_accessed=2 * queries.size, transcendentals=pairs * heads
        ),
        name="attend",
    )(meta, queries, *operands)


def output_kernel(c_ref, w_ref, o_ref):
    o_ref[0] = jnp.dot(c_ref[...], w_ref[...], preferred_element_type=jnp.float32).astype(jnp.bfloat16)


def output_terms(context, out_weight, shards):
    rows, head_width = context.shape
    width = out_weight.shape[1] // shards
    return pl.pallas_call(
        output_kernel,
        grid=(shards,),
        out_shape=jax.ShapeDtypeStruct((shards, rows, width), jnp.bfloat16),
        in_specs=[
            pl.BlockSpec((rows, head_width), lambda z: (0, 0)),
            pl.BlockSpec((head_width, width), lambda z: (0, z)),
        ],
        out_specs=pl.BlockSpec((1, rows, width), lambda z: (z, 0, 0)),
        compiler_params=pltpu.CompilerParams(vmem_limit_bytes=VMEM_LIMIT),
        name="output_terms",
    )(context, out_weight)


def per_device(hidden, depth, qkv_weight, out_weight):
    tokens = hidden[0]
    local_len = tokens.shape[0]
    docs = lax.axis_size("dp")
    ctx_count = lax.axis_size("ctx")
    shards = lax.axis_size("tensor")
    plane = docs * ctx_count
    me = lax.axis_index("dp") * ctx_count + lax.axis_index("ctx")
    size = CAP // plane
    stripes = ACT_DEV // size

    active = depth[0] >= RECURSION
    ones = active.astype(jnp.int32)
    counts = lax.all_gather(jnp.sum(ones)[None], PLANE, axis=0, tiled=True)
    ends = jnp.cumsum(counts)
    starts = ends - counts
    tiles = local_len // TILE
    tile_counts = jnp.sum(ones.reshape(tiles, TILE), axis=1)
    base = lax.rem(starts[me] + jnp.cumsum(tile_counts) - tile_counts, CAP).astype(jnp.int32)
    within = jnp.cumsum(ones.reshape(tiles, TILE), axis=1) - 1
    relative = jnp.where(active.reshape(tiles, TILE), within + lax.rem(base, ALIGN)[:, None], -1)
    relative = relative.reshape(tiles, 1, TILE)
    dealt = deal(base, relative, tokens)
    received = lax.all_to_all(dealt.reshape(plane, size, -1), PLANE, 0, 0)

    index = (
        jnp.arange(stripes, dtype=jnp.int32)[:, None] * CAP
        + me * size
        + jnp.arange(size, dtype=jnp.int32)[None, :]
    )
    owned = (index[None] >= starts[:, None, None]) & (index[None] < ends[:, None, None])
    zero = jnp.zeros((), jnp.bfloat16)
    packed = jnp.where(owned[0][:, :, None], received[0][None], zero)
    for b in range(1, plane):
        packed = jnp.where(owned[b][:, :, None], received[b][None], packed)
    packed = packed.reshape(ACT_DEV, -1)

    chunks = 2
    chunk_stripes = stripes // chunks
    chunk_rows = ACT_DEV // chunks
    weight = jnp.transpose(qkv_weight, (1, 0, 2))
    meta = jnp.concatenate([starts[::ctx_count], me[None]]).astype(jnp.int32)
    rows_all = [
        lax.all_gather(packed[c * chunk_rows : (c + 1) * chunk_rows], "tensor", axis=0) for c in range(chunks)
    ]
    projected = [project(rows_all[c], weight) for c in range(chunks)]
    kvs, backs = [], []
    context = None
    for c in range(chunks):
        queries, kv = projected[c]
        blocks, context = gather_plane(kv, context)
        if c > 0:
            terms = output_terms(context, out_weight, shards)
            backs.append(lax.psum_scatter(terms, "tensor", scatter_dimension=0))
        kvs = kvs + blocks
        if c + 1 < chunks:
            queries, ahead = lax.optimization_barrier((queries, projected[c + 1][1]))
            projected[c + 1] = (projected[c + 1][0], ahead)
        context = attend(meta, queries, kvs, c, docs, chunk_stripes, CAP)
    terms = output_terms(context, out_weight, shards)
    backs.append(lax.psum_scatter(terms, "tensor", scatter_dimension=0))
    rows_back = jnp.concatenate(backs, axis=0)

    rows_back = rows_back.reshape(stripes, size, -1)
    returned = jnp.where(owned[:, 0][:, :, None], rows_back[0][None], zero)
    for k in range(1, stripes):
        returned = jnp.where(owned[:, k][:, :, None], rows_back[k][None], returned)
    landed = lax.all_to_all(returned, PLANE, 0, 0).reshape(CAP, -1)
    update = spread(base, relative, landed)
    return update[None]


def solution(mesh):
    placed = (P("dp", "ctx", "tensor"), P("dp", "ctx"), P(None, None, "tensor"), P("tensor", None))
    return jax.shard_map(
        per_device, mesh=mesh, in_specs=placed, out_specs=P("dp", "ctx", "tensor"), check_vma=False
    )
```

```python
import functools

import jax
import jax.numpy as jnp
from jax import lax
from jax.experimental import pallas as pl
from jax.experimental.pallas import tpu as pltpu
from jax.sharding import PartitionSpec as P

HD = 128
RECURSION = 3
CAP = 1024
ACT_DEV = 512

score_scale = 0.25
norm_epsilon = 1e-05
head_epsilon = 1e-06
VMEM_LIMIT = 60 * 1024 * 1024
PLANE = ("dp", "ctx")


def exchange_kernel(plane, x_ref, o_ref, send_sem, recv_sem, local_sem):
    ctx_count = lax.axis_size("ctx")
    me = lax.axis_index("dp") * ctx_count + lax.axis_index("ctx")

    def device(place):
        return {"dp": place // ctx_count, "ctx": lax.rem(place, ctx_count)}

    barrier = pltpu.get_barrier_semaphore()
    for step in range(1, plane):
        target = device(lax.rem(me + step, plane))
        pl.semaphore_signal(barrier, inc=1, device_id=target, device_id_type=pl.DeviceIdType.MESH)
    pl.semaphore_wait(barrier, plane - 1)

    sends = []
    for step in range(1, plane):
        place = lax.rem(me + step, plane)
        copy = pltpu.make_async_remote_copy(
            src_ref=x_ref.at[place],
            dst_ref=o_ref.at[me],
            send_sem=send_sem.at[step],
            recv_sem=recv_sem.at[step],
            device_id=device(place),
            device_id_type=pl.DeviceIdType.MESH,
        )
        copy.start()
        sends.append(copy)
    local = pltpu.make_async_copy(x_ref.at[me], o_ref.at[me], local_sem)
    local.start()
    for step in range(1, plane):
        origin = lax.rem(me + plane - step, plane)
        pltpu.make_async_remote_copy(
            src_ref=x_ref.at[origin],
            dst_ref=o_ref.at[origin],
            send_sem=send_sem.at[step],
            recv_sem=recv_sem.at[step],
            device_id=device(origin),
            device_id_type=pl.DeviceIdType.MESH,
        ).wait_recv()
    for copy in sends:
        copy.wait_send()
    local.wait()


def exchange(x, call):
    plane = x.shape[0]
    return pl.pallas_call(
        functools.partial(exchange_kernel, plane),
        out_shape=jax.ShapeDtypeStruct(x.shape, x.dtype),
        in_specs=[pl.BlockSpec(memory_space=pltpu.VMEM)],
        out_specs=pl.BlockSpec(memory_space=pltpu.VMEM),
        scratch_shapes=[
            pltpu.SemaphoreType.DMA((plane,)),
            pltpu.SemaphoreType.DMA((plane,)),
            pltpu.SemaphoreType.DMA,
        ],
        compiler_params=pltpu.CompilerParams(collective_id=call, has_side_effects=True),
        name="exchange",
    )(x)


def project_kernel(x_ref, w_ref, q_ref, kv_ref, normed):
    part = pl.program_id(0)
    shards, rows, width = x_ref.shape

    @pl.when(part == 0)
    def _():
        total = jnp.zeros((rows, 1), jnp.float32)
        for z in range(shards):
            wide = x_ref[z].astype(jnp.float32)
            total = total + jnp.sum(wide * wide, axis=1, keepdims=True)
        factor = lax.rsqrt(total / (shards * width) + norm_epsilon)
        for z in range(shards):
            normed[z] = (x_ref[z].astype(jnp.float32) * factor).astype(jnp.bfloat16)

    acc = jnp.dot(normed[0], w_ref[0, :width], preferred_element_type=jnp.float32)
    for z in range(1, shards):
        acc = acc + jnp.dot(normed[z], w_ref[0, z * width : (z + 1) * width], preferred_element_type=jnp.float32)
    heads = acc.shape[1] // HD

    def head_normed(scale):
        parts = []
        for h in range(heads):
            head = acc[:, h * HD : (h + 1) * HD]
            factor = lax.rsqrt(jnp.mean(head * head, axis=1, keepdims=True) + head_epsilon) * scale
            parts.append((head * factor).astype(jnp.bfloat16))
        return parts

    @pl.when(part == 0)
    def _():
        for h, value in enumerate(head_normed(score_scale)):
            q_ref[:, h * HD : (h + 1) * HD] = value

    @pl.when(part == 1)
    def _():
        for h, value in enumerate(head_normed(1.0)):
            kv_ref[0, :, h * HD : (h + 1) * HD] = value

    @pl.when(part == 2)
    def _():
        kv_ref[0] = acc.astype(jnp.bfloat16)


def project(rows_all, weight):
    shards, rows, width = rows_all.shape
    head_width = weight.shape[2]
    flops = 2 * rows * shards * width * 3 * head_width
    return pl.pallas_call(
        project_kernel,
        grid=(3,),
        out_shape=[
            jax.ShapeDtypeStruct((rows, head_width), jnp.bfloat16),
            jax.ShapeDtypeStruct((2, rows, head_width), jnp.bfloat16),
        ],
        in_specs=[
            pl.BlockSpec((shards, rows, width), lambda p: (0, 0, 0)),
            pl.BlockSpec((1, shards * width, head_width), lambda p: (p, 0, 0)),
        ],
        out_specs=[
            pl.BlockSpec((rows, head_width), lambda p: (0, 0)),
            pl.BlockSpec((1, rows, head_width), lambda p: (jnp.maximum(p - 1, 0), 0, 0)),
        ],
        scratch_shapes=[pltpu.VMEM((shards, rows, width), jnp.bfloat16)],
        compiler_params=pltpu.CompilerParams(vmem_limit_bytes=VMEM_LIMIT),
        cost_estimate=pl.CostEstimate(flops=flops, bytes_accessed=2 * weight.size, transcendentals=0),
        name="project",
    )(rows_all, weight)


def gather_kernel(pieces, kv_ref, out_ref, send_sem, recv_sem, local_sem):
    x, place = lax.axis_index("dp"), lax.axis_index("ctx")
    y, core = place // 2, lax.rem(place, 2)
    rows = kv_ref.shape[1] // pieces

    def block(flip_x, flip_y, flip_core):
        return (x ^ flip_x) * 4 + (y ^ flip_y) * 2 + (core ^ flip_core)

    def device(flip_x, flip_y, flip_core):
        return {"dp": x ^ flip_x, "ctx": (y ^ flip_y) * 2 + (core ^ flip_core)}

    sibling, across_x, across_y = device(0, 0, 1), device(1, 0, 0), device(0, 1, 0)
    barrier = pltpu.get_barrier_semaphore()
    for target in (sibling, across_x, across_y):
        pl.semaphore_signal(barrier, inc=1, device_id=target, device_id_type=pl.DeviceIdType.MESH)
    pl.semaphore_wait(barrier, 3)

    me = block(0, 0, 0)
    local = pltpu.make_async_copy(kv_ref, out_ref.at[me], local_sem)
    local.start()
    sends = []

    def send(origin, route, piece, target, own=False):
        window = pl.ds(piece * rows, rows)
        copy = pltpu.make_async_remote_copy(
            src_ref=kv_ref.at[:, window] if own else out_ref.at[origin, :, window],
            dst_ref=out_ref.at[origin, :, window],
            send_sem=send_sem.at[route, piece],
            recv_sem=recv_sem.at[route, piece],
            device_id=target,
            device_id_type=pl.DeviceIdType.MESH,
        )
        copy.start()
        sends.append(copy)

    def arrive(origin, route, piece):
        window = pl.ds(piece * rows, rows)
        pltpu.make_async_remote_copy(
            src_ref=out_ref.at[origin, :, window],
            dst_ref=out_ref.at[origin, :, window],
            send_sem=send_sem.at[route, piece],
            recv_sem=recv_sem.at[route, piece],
            device_id=sibling,
            device_id_type=pl.DeviceIdType.MESH,
        ).wait_recv()

    for piece in range(pieces):
        send(me, 1, piece, across_x, True)
        send(me, 2, piece, across_y, True)
        send(me, 0, piece, sibling, True)
    first = core == 0
    onward = jnp.where(first, block(0, 1, 0), block(1, 0, 0))
    onward_device = {
        "dp": jnp.where(first, x ^ 1, x),
        "ctx": jnp.where(first, place, (y ^ 1) * 2 + core),
    }
    for piece in range(pieces):
        arrive(block(1, 0, 0), 1, piece)
        arrive(block(0, 1, 0), 2, piece)
        send(onward, 3, piece, onward_device)
        send(block(1, 0, 0), 4, piece, sibling)
        send(block(0, 1, 0), 5, piece, sibling)
    for piece in range(pieces):
        arrive(block(1, 1, 0), 3, piece)
        send(block(1, 1, 0), 6, piece, sibling)
    for piece in range(pieces):
        arrive(block(0, 0, 1), 0, piece)
        arrive(block(1, 0, 1), 4, piece)
        arrive(block(0, 1, 1), 5, piece)
        arrive(block(1, 1, 1), 6, piece)
    for copy in sends:
        copy.wait_send()
    local.wait()


def gather_plane(kv, call):
    docs, ctx_count = lax.axis_size("dp"), lax.axis_size("ctx")
    if (docs, ctx_count) != (2, 4):
        return lax.all_gather(kv, PLANE, axis=0)
    pieces = 4
    plane = docs * ctx_count
    return pl.pallas_call(
        functools.partial(gather_kernel, pieces),
        out_shape=jax.ShapeDtypeStruct((plane,) + kv.shape, kv.dtype),
        in_specs=[pl.BlockSpec(memory_space=pltpu.VMEM)],
        out_specs=pl.BlockSpec(memory_space=pl.ANY),
        scratch_shapes=[
            pltpu.SemaphoreType.DMA((7, pieces)),
            pltpu.SemaphoreType.DMA((7, pieces)),
            pltpu.SemaphoreType.DMA,
        ],
        compiler_params=pltpu.CompilerParams(collective_id=call, has_side_effects=True),
        cost_estimate=pl.CostEstimate(flops=0, bytes_accessed=60_000_000, transcendentals=0),
        name="gather_plane",
    )(kv)


def attend_kernel(docs, base, meta_ref, q_ref, *refs):
    o_ref = refs[-1]
    pairs = [(refs[i], refs[i + 1]) for i in range(0, len(refs) - 1, 2)]
    plane, stripes, size, _ = refs[0].shape
    period = plane * size
    rows = stripes * size
    me = meta_ref[docs]
    row = lax.broadcasted_iota(jnp.int32, (rows, 1), 0)
    q_index = (base + row // size) * period + me * size + lax.rem(row, size)
    begin = jnp.zeros((rows, 1), jnp.int32)
    for d in range(docs):
        begin = jnp.where(q_index >= meta_ref[d], meta_ref[d], begin)
    lane = lax.broadcasted_iota(jnp.int32, (1, period), 1)
    query = q_ref[...]
    num = jnp.zeros((rows, HD), jnp.float32)
    den = jnp.zeros((rows, 1), jnp.float32)
    at = 0
    for k_ref, v_ref in pairs:
        for k in range(stripes):
            keys = k_ref[:, k].reshape(period, HD)
            values = v_ref[:, k].reshape(period, HD)
            scores = lax.dot_general(query, keys, (((1,), (1,)), ((), ())), preferred_element_type=jnp.float32)
            allowed = lane >= begin - at * period
            if at >= base:
                allowed = allowed & (lane <= q_index - at * period)
            weights = jnp.where(allowed, jnp.exp(scores), 0.0)
            den = den + jnp.sum(weights, axis=1, keepdims=True)
            num = num + jnp.dot(weights.astype(jnp.bfloat16), values, preferred_element_type=jnp.float32)
            at += 1
    o_ref[...] = (num / den).astype(jnp.bfloat16)


def attend(meta, queries, kvs, docs, stripes):
    rows, head_width = queries.shape
    plane = kvs[0].shape[0]
    size = rows // stripes
    heads = head_width // HD
    operands, specs = [], []
    for kv in kvs:
        kv = kv.reshape(plane, 2, stripes, size, head_width)
        for which in range(2):
            operands.append(kv)
            specs.append(
                pl.BlockSpec((plane, None, stripes, size, HD), lambda h, m, which=which: (0, which, 0, 0, h))
            )
    pairs = rows * plane * rows * len(kvs)
    return pl.pallas_call(
        functools.partial(attend_kernel, docs, (len(kvs) - 1) * stripes),
        grid_spec=pltpu.PrefetchScalarGridSpec(
            num_scalar_prefetch=1,
            grid=(heads,),
            in_specs=[pl.BlockSpec((rows, HD), lambda h, m: (0, h))] + specs,
            out_specs=pl.BlockSpec((rows, HD), lambda h, m: (0, h)),
        ),
        out_shape=jax.ShapeDtypeStruct((rows, head_width), jnp.bfloat16),
        compiler_params=pltpu.CompilerParams(vmem_limit_bytes=VMEM_LIMIT),
        cost_estimate=pl.CostEstimate(
            flops=4 * pairs * head_width, bytes_accessed=4 * kvs[0].size, transcendentals=pairs * heads
        ),
        name="attend",
    )(meta, queries, *operands)


def output_kernel(c_ref, w_ref, o_ref):
    o_ref[0] = jnp.dot(c_ref[...], w_ref[...], preferred_element_type=jnp.float32).astype(jnp.bfloat16)


def output_terms(context, out_weight, shards):
    rows, head_width = context.shape
    width = out_weight.shape[1] // shards
    return pl.pallas_call(
        output_kernel,
        grid=(shards,),
        out_shape=jax.ShapeDtypeStruct((shards, rows, width), jnp.bfloat16),
        in_specs=[
            pl.BlockSpec((rows, head_width), lambda z: (0, 0)),
            pl.BlockSpec((head_width, width), lambda z: (0, z)),
        ],
        out_specs=pl.BlockSpec((1, rows, width), lambda z: (z, 0, 0)),
        compiler_params=pltpu.CompilerParams(vmem_limit_bytes=VMEM_LIMIT),
        name="output_terms",
    )(context, out_weight)


def per_device(hidden, depth, qkv_weight, out_weight):
    tokens = hidden[0]
    local_len = tokens.shape[0]
    docs = lax.axis_size("dp")
    ctx_count = lax.axis_size("ctx")
    shards = lax.axis_size("tensor")
    plane = docs * ctx_count
    me = lax.axis_index("dp") * ctx_count + lax.axis_index("ctx")
    size = CAP // plane
    stripes = ACT_DEV // size

    active = depth[0] >= RECURSION
    ones = active.astype(jnp.int32)
    counts = exchange(jnp.broadcast_to(jnp.sum(ones), (plane, 8, HD)), 2)[:, 0, 0]
    ends = jnp.cumsum(counts)
    starts = ends - counts
    rank = jnp.cumsum(ones) - 1
    slot = jnp.where(active, lax.rem(starts[me] + rank, CAP), -1)
    onehot = (jnp.arange(CAP, dtype=jnp.int32)[:, None] == slot[None, :]).astype(jnp.bfloat16)
    dealt = jnp.dot(onehot, tokens, preferred_element_type=jnp.float32).astype(jnp.bfloat16)
    received = exchange(dealt.reshape(plane, size, -1), 3)

    index = (
        jnp.arange(stripes, dtype=jnp.int32)[:, None] * CAP
        + me * size
        + jnp.arange(size, dtype=jnp.int32)[None, :]
    )
    owned = (index[None] >= starts[:, None, None]) & (index[None] < ends[:, None, None])
    zero = jnp.zeros((), jnp.bfloat16)
    packed = jnp.where(owned[0][:, :, None], received[0][None], zero)
    for b in range(1, plane):
        packed = jnp.where(owned[b][:, :, None], received[b][None], packed)
    packed = packed.reshape(ACT_DEV, -1)

    chunks = 2
    chunk_stripes = stripes // chunks
    chunk_rows = ACT_DEV // chunks
    weight = jnp.transpose(qkv_weight, (1, 0, 2))
    meta = jnp.concatenate([starts[::ctx_count], me[None]]).astype(jnp.int32)
    rows_all = [
        lax.all_gather(packed[c * chunk_rows : (c + 1) * chunk_rows], "tensor", axis=0) for c in range(chunks)
    ]
    kvs, backs = [], []
    for c in range(chunks):
        queries, kv = project(rows_all[c], weight)
        kvs.append(gather_plane(kv, c))
        context = attend(meta, queries, kvs, docs, chunk_stripes)
        terms = output_terms(context, out_weight, shards)
        backs.append(lax.psum_scatter(terms, "tensor", scatter_dimension=0))
    rows_back = jnp.concatenate(backs, axis=0)

    rows_back = rows_back.reshape(stripes, size, -1)
    returned = jnp.where(owned[:, 0][:, :, None], rows_back[0][None], zero)
    for k in range(1, stripes):
        returned = jnp.where(owned[:, k][:, :, None], rows_back[k][None], returned)
    landed = exchange(returned, 4).reshape(CAP, -1)
    spread = (slot[:, None] == jnp.arange(CAP, dtype=jnp.int32)[None, :]).astype(jnp.bfloat16)
    update = jnp.dot(spread, landed, preferred_element_type=jnp.float32).astype(jnp.bfloat16)
    return update[None]


def solution(mesh):
    placed = (P("dp", "ctx", "tensor"), P("dp", "ctx"), P(None, None, "tensor"), P("tensor", None))
    return jax.shard_map(
        per_device, mesh=mesh, in_specs=placed, out_specs=P("dp", "ctx", "tensor"), check_vma=False
    )
```

```python
import functools

import jax
import jax.numpy as jnp
from jax import lax
from jax.experimental import pallas as pl
from jax.experimental.pallas import tpu as pltpu
from jax.sharding import PartitionSpec as P

HD = 128
RECURSION = 3
CAP = 1024
ACT_DEV = 512

score_scale = 0.25
norm_epsilon = 1e-05
head_epsilon = 1e-06
VMEM_LIMIT = 60 * 1024 * 1024
PLANE = ("dp", "ctx")


def project_kernel(x_ref, w_ref, q_ref, kv_ref, normed):
    part = pl.program_id(0)
    shards, rows, width = x_ref.shape

    @pl.when(part == 0)
    def _():
        total = jnp.zeros((rows, 1), jnp.float32)
        for z in range(shards):
            wide = x_ref[z].astype(jnp.float32)
            total = total + jnp.sum(wide * wide, axis=1, keepdims=True)
        factor = lax.rsqrt(total / (shards * width) + norm_epsilon)
        for z in range(shards):
            normed[z] = (x_ref[z].astype(jnp.float32) * factor).astype(jnp.bfloat16)

    acc = jnp.dot(normed[0], w_ref[0, :width], preferred_element_type=jnp.float32)
    for z in range(1, shards):
        acc = acc + jnp.dot(normed[z], w_ref[0, z * width : (z + 1) * width], preferred_element_type=jnp.float32)
    heads = acc.shape[1] // HD

    def head_normed(scale):
        parts = []
        for h in range(heads):
            head = acc[:, h * HD : (h + 1) * HD]
            factor = lax.rsqrt(jnp.mean(head * head, axis=1, keepdims=True) + head_epsilon) * scale
            parts.append((head * factor).astype(jnp.bfloat16))
        return parts

    @pl.when(part == 0)
    def _():
        for h, value in enumerate(head_normed(score_scale)):
            q_ref[:, h * HD : (h + 1) * HD] = value

    @pl.when(part == 1)
    def _():
        for h, value in enumerate(head_normed(1.0)):
            kv_ref[0, :, h * HD : (h + 1) * HD] = value

    @pl.when(part == 2)
    def _():
        kv_ref[0] = acc.astype(jnp.bfloat16)


def project(rows_all, weight):
    shards, rows, width = rows_all.shape
    head_width = weight.shape[2]
    flops = 2 * rows * shards * width * 3 * head_width
    return pl.pallas_call(
        project_kernel,
        grid=(3,),
        out_shape=[
            jax.ShapeDtypeStruct((rows, head_width), jnp.bfloat16),
            jax.ShapeDtypeStruct((2, rows, head_width), jnp.bfloat16),
        ],
        in_specs=[
            pl.BlockSpec((shards, rows, width), lambda p: (0, 0, 0)),
            pl.BlockSpec((1, shards * width, head_width), lambda p: (p, 0, 0)),
        ],
        out_specs=[
            pl.BlockSpec((rows, head_width), lambda p: (0, 0)),
            pl.BlockSpec((1, rows, head_width), lambda p: (jnp.maximum(p - 1, 0), 0, 0)),
        ],
        scratch_shapes=[pltpu.VMEM((shards, rows, width), jnp.bfloat16)],
        compiler_params=pltpu.CompilerParams(vmem_limit_bytes=VMEM_LIMIT),
        cost_estimate=pl.CostEstimate(flops=flops, bytes_accessed=2 * weight.size, transcendentals=0),
        name="project",
    )(rows_all, weight)


def gather_kernel(pieces, kv_ref, out_ref, send_sem, recv_sem, local_sem):
    x, place = lax.axis_index("dp"), lax.axis_index("ctx")
    y, core = place // 2, lax.rem(place, 2)
    rows = kv_ref.shape[1] // pieces

    def block(flip_x, flip_y, flip_core):
        return (x ^ flip_x) * 4 + (y ^ flip_y) * 2 + (core ^ flip_core)

    def device(flip_x, flip_y, flip_core):
        return {"dp": x ^ flip_x, "ctx": (y ^ flip_y) * 2 + (core ^ flip_core)}

    sibling, across_x, across_y = device(0, 0, 1), device(1, 0, 0), device(0, 1, 0)
    barrier = pltpu.get_barrier_semaphore()
    for target in (sibling, across_x, across_y):
        pl.semaphore_signal(barrier, inc=1, device_id=target, device_id_type=pl.DeviceIdType.MESH)
    pl.semaphore_wait(barrier, 3)

    me = block(0, 0, 0)
    local = pltpu.make_async_copy(kv_ref, out_ref.at[me], local_sem)
    local.start()
    sends = []

    def send(origin, route, piece, target, own=False):
        window = pl.ds(piece * rows, rows)
        copy = pltpu.make_async_remote_copy(
            src_ref=kv_ref.at[:, window] if own else out_ref.at[origin, :, window],
            dst_ref=out_ref.at[origin, :, window],
            send_sem=send_sem.at[route, piece],
            recv_sem=recv_sem.at[route, piece],
            device_id=target,
            device_id_type=pl.DeviceIdType.MESH,
        )
        copy.start()
        sends.append(copy)

    def arrive(origin, route, piece):
        window = pl.ds(piece * rows, rows)
        pltpu.make_async_remote_copy(
            src_ref=out_ref.at[origin, :, window],
            dst_ref=out_ref.at[origin, :, window],
            send_sem=send_sem.at[route, piece],
            recv_sem=recv_sem.at[route, piece],
            device_id=sibling,
            device_id_type=pl.DeviceIdType.MESH,
        ).wait_recv()

    for piece in range(pieces):
        send(me, 1, piece, across_x, True)
        send(me, 2, piece, across_y, True)
        send(me, 0, piece, sibling, True)
    first = core == 0
    onward = jnp.where(first, block(0, 1, 0), block(1, 0, 0))
    onward_device = {
        "dp": jnp.where(first, x ^ 1, x),
        "ctx": jnp.where(first, place, (y ^ 1) * 2 + core),
    }
    for piece in range(pieces):
        arrive(block(1, 0, 0), 1, piece)
        arrive(block(0, 1, 0), 2, piece)
        send(onward, 3, piece, onward_device)
        send(block(1, 0, 0), 4, piece, sibling)
        send(block(0, 1, 0), 5, piece, sibling)
    for piece in range(pieces):
        arrive(block(1, 1, 0), 3, piece)
        send(block(1, 1, 0), 6, piece, sibling)
    for piece in range(pieces):
        arrive(block(0, 0, 1), 0, piece)
        arrive(block(1, 0, 1), 4, piece)
        arrive(block(0, 1, 1), 5, piece)
        arrive(block(1, 1, 1), 6, piece)
    for copy in sends:
        copy.wait_send()
    local.wait()


def gather_plane(kv, call):
    docs, ctx_count = lax.axis_size("dp"), lax.axis_size("ctx")
    if (docs, ctx_count) != (2, 4):
        return lax.all_gather(kv, PLANE, axis=0)
    pieces = 8
    plane = docs * ctx_count
    return pl.pallas_call(
        functools.partial(gather_kernel, pieces),
        out_shape=jax.ShapeDtypeStruct((plane,) + kv.shape, kv.dtype),
        in_specs=[pl.BlockSpec(memory_space=pltpu.VMEM)],
        out_specs=pl.BlockSpec(memory_space=pl.ANY),
        scratch_shapes=[
            pltpu.SemaphoreType.DMA((7, pieces)),
            pltpu.SemaphoreType.DMA((7, pieces)),
            pltpu.SemaphoreType.DMA,
        ],
        compiler_params=pltpu.CompilerParams(collective_id=call, has_side_effects=True),
        cost_estimate=pl.CostEstimate(flops=0, bytes_accessed=60_000_000, transcendentals=0),
        name="gather_plane",
    )(kv)


def attend_kernel(docs, base, meta_ref, q_ref, *refs):
    w_ref, o_ref, total = refs[-3:]
    pairs = [(refs[i], refs[i + 1]) for i in range(0, len(refs) - 3, 2)]
    head = pl.program_id(0)
    plane, stripes, size, _ = refs[0].shape
    period = plane * size
    rows = stripes * size
    me = meta_ref[docs]
    row = lax.broadcasted_iota(jnp.int32, (rows, 1), 0)
    q_index = (base + row // size) * period + me * size + lax.rem(row, size)
    begin = jnp.zeros((rows, 1), jnp.int32)
    for d in range(docs):
        begin = jnp.where(q_index >= meta_ref[d], meta_ref[d], begin)
    lane = lax.broadcasted_iota(jnp.int32, (1, period), 1)
    query = q_ref[...]
    num = jnp.zeros((rows, HD), jnp.float32)
    den = jnp.zeros((rows, 1), jnp.float32)
    at = 0
    for k_ref, v_ref in pairs:
        for k in range(stripes):
            keys = k_ref[:, k].reshape(period, HD)
            values = v_ref[:, k].reshape(period, HD)
            scores = lax.dot_general(query, keys, (((1,), (1,)), ((), ())), preferred_element_type=jnp.float32)
            allowed = lane >= begin - at * period
            if at >= base:
                allowed = allowed & (lane <= q_index - at * period)
            weights = jnp.where(allowed, jnp.exp(scores), 0.0)
            den = den + jnp.sum(weights, axis=1, keepdims=True)
            num = num + jnp.dot(weights.astype(jnp.bfloat16), values, preferred_element_type=jnp.float32)
            at += 1
    context = (num / den).astype(jnp.bfloat16)
    term = jnp.dot(context, w_ref[...], preferred_element_type=jnp.float32)

    @pl.when(head == 0)
    def _():
        total[...] = term

    @pl.when(head > 0)
    def _():
        total[...] += term

    @pl.when(head == pl.num_programs(0) - 1)
    def _():
        width = o_ref.shape[2]
        for z in range(o_ref.shape[0]):
            o_ref[z] = total[:, z * width : (z + 1) * width].astype(jnp.bfloat16)


def attend(meta, queries, kvs, out_weight, shards, docs, stripes):
    rows, head_width = queries.shape
    plane = kvs[0].shape[0]
    size = rows // stripes
    heads = head_width // HD
    operands, specs = [], []
    for kv in kvs:
        kv = kv.reshape(plane, 2, stripes, size, head_width)
        for which in range(2):
            operands.append(kv)
            specs.append(
                pl.BlockSpec((plane, None, stripes, size, HD), lambda h, m, which=which: (0, which, 0, 0, h))
            )
    width = out_weight.shape[1]
    operands.append(out_weight)
    specs.append(pl.BlockSpec((HD, width), lambda h, m: (h, 0)))
    pairs = rows * plane * rows * len(kvs)
    return pl.pallas_call(
        functools.partial(attend_kernel, docs, (len(kvs) - 1) * stripes),
        grid_spec=pltpu.PrefetchScalarGridSpec(
            num_scalar_prefetch=1,
            grid=(heads,),
            in_specs=[pl.BlockSpec((rows, HD), lambda h, m: (0, h))] + specs,
            out_specs=pl.BlockSpec((shards, rows, width // shards), lambda h, m: (0, 0, 0)),
            scratch_shapes=[pltpu.VMEM((rows, width), jnp.float32)],
        ),
        out_shape=jax.ShapeDtypeStruct((shards, rows, width // shards), jnp.bfloat16),
        compiler_params=pltpu.CompilerParams(vmem_limit_bytes=VMEM_LIMIT),
        cost_estimate=pl.CostEstimate(
            flops=4 * pairs * head_width, bytes_accessed=4 * kvs[0].size, transcendentals=pairs * heads
        ),
        name="attend",
    )(meta, queries, *operands)


def per_device(hidden, depth, qkv_weight, out_weight):
    tokens = hidden[0]
    local_len = tokens.shape[0]
    docs = lax.axis_size("dp")
    ctx_count = lax.axis_size("ctx")
    shards = lax.axis_size("tensor")
    plane = docs * ctx_count
    me = lax.axis_index("dp") * ctx_count + lax.axis_index("ctx")
    size = CAP // plane
    stripes = ACT_DEV // size

    active = depth[0] >= RECURSION
    ones = active.astype(jnp.int32)
    counts = lax.all_gather(jnp.sum(ones)[None], PLANE, axis=0, tiled=True)
    ends = jnp.cumsum(counts)
    starts = ends - counts
    rank = jnp.cumsum(ones) - 1
    slot = jnp.where(active, lax.rem(starts[me] + rank, CAP), -1)
    onehot = (jnp.arange(CAP, dtype=jnp.int32)[:, None] == slot[None, :]).astype(jnp.bfloat16)
    dealt = jnp.dot(onehot, tokens, preferred_element_type=jnp.float32).astype(jnp.bfloat16)
    received = lax.all_to_all(dealt.reshape(plane, size, -1), PLANE, 0, 0)

    index = (
        jnp.arange(stripes, dtype=jnp.int32)[:, None] * CAP
        + me * size
        + jnp.arange(size, dtype=jnp.int32)[None, :]
    )
    owned = (index[None] >= starts[:, None, None]) & (index[None] < ends[:, None, None])
    zero = jnp.zeros((), jnp.bfloat16)
    packed = jnp.where(owned[0][:, :, None], received[0][None], zero)
    for b in range(1, plane):
        packed = jnp.where(owned[b][:, :, None], received[b][None], packed)
    packed = packed.reshape(ACT_DEV, -1)

    chunks = 2
    chunk_stripes = stripes // chunks
    chunk_rows = ACT_DEV // chunks
    weight = jnp.transpose(qkv_weight, (1, 0, 2))
    meta = jnp.concatenate([starts[::ctx_count], me[None]]).astype(jnp.int32)
    rows_all = [
        lax.all_gather(packed[c * chunk_rows : (c + 1) * chunk_rows], "tensor", axis=0) for c in range(chunks)
    ]
    kvs, backs = [], []
    for c in range(chunks):
        queries, kv = project(rows_all[c], weight)
        kvs.append(gather_plane(kv, c))
        terms = attend(meta, queries, kvs, out_weight, shards, docs, chunk_stripes)
        backs.append(lax.psum_scatter(terms, "tensor", scatter_dimension=0))
    rows_back = jnp.concatenate(backs, axis=0)

    rows_back = rows_back.reshape(stripes, size, -1)
    returned = jnp.where(owned[:, 0][:, :, None], rows_back[0][None], zero)
    for k in range(1, stripes):
        returned = jnp.where(owned[:, k][:, :, None], rows_back[k][None], returned)
    landed = lax.all_to_all(returned, PLANE, 0, 0).reshape(CAP, -1)
    spread = (slot[:, None] == jnp.arange(CAP, dtype=jnp.int32)[None, :]).astype(jnp.bfloat16)
    update = jnp.dot(spread, landed, preferred_element_type=jnp.float32).astype(jnp.bfloat16)
    return update[None]


def solution(mesh):
    placed = (P("dp", "ctx", "tensor"), P("dp", "ctx"), P(None, None, "tensor"), P("tensor", None))
    return jax.shard_map(
        per_device, mesh=mesh, in_specs=placed, out_specs=P("dp", "ctx", "tensor"), check_vma=False
    )
```
